32 devices in a mesh: rows: 8 (over z, y), cls: 4 (over x, core).
Axes of the slice: x: 2, y: 2, z: 4, core: 2. Of those that a mesh axis runs over, the one named last changes fastest.
Arguments:
- features: bfloat16 [6144, 2048], P('rows', 'cls'), may hold values from -32 to 32
- prototypes: bfloat16 [2048, 16384], P('rows', 'cls'), may hold values from -1 to 1
Outputs:
- grad_proto: float32 [2048, 16384], P('rows', 'cls')
The draws below stay inside these ranges and needn't reach their ends.
All inputs are finite; a program needn't handle non-finite values.
Results may differ from the reference program's by a relative error of at most 0.02.
Values may be sent and summed in bfloat16 or wider, within the bound.
A program may use at most 128 MiB of HBM per device.

```python
import jax
import jax.numpy as jnp
from jax import lax

D = 2048
K = 16384
B_DEV = 768
ITERS = 3
BATCH = 6144


def proto_matrix(key):
    proto_key = jax.random.fold_in(key, 101)
    base = jnp.clip(jax.random.normal(proto_key, (D, K), jnp.float32), -5.0, 5.0)
    return (base * D ** (-0.5)).astype(jnp.bfloat16).astype(jnp.float32)


def draw_prototypes(key, part):
    return proto_matrix(key).astype(jnp.bfloat16)


def draw_features(key, part):
    key_list = [jax.random.fold_in(key, 200 + index) for index in range(8)]
    blocks = BATCH // B_DEV
    block_width = D // blocks
    values = jnp.clip(jax.random.normal(key_list[0], (BATCH, D), jnp.float32), -4.0, 4.0)
    pairing = jax.random.permutation(key_list[3], blocks)
    row_block = jnp.arange(BATCH) // B_DEV
    col_block = jnp.arange(D) // block_width
    spike = jnp.where(col_block[None, :] == pairing[row_block][:, None], 3.0, 1.0)
    values = values * spike
    return jnp.clip(values, -32.0, 32.0).astype(jnp.bfloat16)


def setup_inputs(seed: int = 0) -> dict:
    key_of = jax.random.split(jax.random.key(seed), 3)
    features = draw_features(jax.random.fold_in(key_of[2], 71), 0)
    prototypes = draw_prototypes(jax.random.fold_in(key_of[2], 71), 0)
    return {"features": features, "prototypes": prototypes}


code_temp = 0.2
loss_temp = 0.3


def reference(features, prototypes):
    num_blocks = features.shape[0] // B_DEV
    classes = prototypes.shape[1]
    feat_blocks = features.reshape(num_blocks, B_DEV, features.shape[1])

    def first_pass(row_block):
        scores = jnp.dot(row_block, prototypes, preferred_element_type=jnp.float32)
        row_top = jnp.max(scores, axis=1, keepdims=True)
        exp_codes = jnp.exp((scores - row_top) / code_temp)
        soft_total = jnp.sum(jnp.exp((scores - row_top) / loss_temp), axis=1)
        return exp_codes, jnp.sum(exp_codes, axis=1), row_top[:, 0], soft_total

    exp_codes, sink_total, row_tops, soft_totals = lax.map(first_pass, feat_blocks)
    row_scale = 1.0 / sink_total
    col_scale = jnp.ones((classes,), jnp.float32)
    balance_ratio = jnp.float32(num_blocks * B_DEV) / jnp.float32(classes)
    for sweep in range(ITERS):
        col_mass = jnp.einsum("bi,bij->j", row_scale, exp_codes, precision=lax.Precision.HIGHEST) * col_scale
        col_scale = col_scale * balance_ratio / col_mass
        row_mass = jnp.einsum("bij,j->bi", exp_codes, col_scale, precision=lax.Precision.HIGHEST) * row_scale
        row_scale = row_scale / row_mass

    def grad_step(running, carried):
        row_block, exp_block, scale_rows, top_rows, soft_rows = carried
        scores = jnp.dot(row_block, prototypes, preferred_element_type=jnp.float32)
        probs_loss = jnp.exp((scores - top_rows[:, None]) / loss_temp) / soft_rows[:, None]
        codes = scale_rows[:, None] * exp_block * col_scale[None, :]
        slope = ((probs_loss - codes) / loss_temp).astype(jnp.bfloat16)
        partial_value = jnp.dot(row_block.T, slope, preferred_element_type=jnp.float32).astype(jnp.bfloat16)
        partial_value = lax.optimization_barrier(partial_value)
        return running + partial_value.astype(jnp.float32), None

    start_grad = jnp.zeros((features.shape[1], classes), jnp.float32)
    grad_proto, _ = lax.scan(grad_step, start_grad, (feat_blocks, exp_codes, row_scale, row_tops, soft_totals))
    return grad_proto
```

```python
import functools

import jax
import jax.numpy as jnp
from jax import lax
from jax.experimental import pallas as pl
from jax.experimental.pallas import tpu as pltpu
from jax.sharding import PartitionSpec as P

ITERS = 3
code_temp = 0.2
loss_temp = 0.3

MESH = pl.DeviceIdType.MESH
F32 = jnp.float32
BF16 = jnp.bfloat16


def snake(p):
    return 2 * (p // 2) + (p + p // 2) % 2


def kernel(
    R, C, feat, protos, out, G, Pb, PT, S, E, SL, GT, fbuf, sendb, st0, st1, a1, a2, b1, b2, q0, q1, res0, res1, wv, av, fv, cs,
    lsem, psend, precv, rs_s, rs_r, ls_s, ls_r, c_s, c_r, x1s, x1r, x2s, x2r, x3s, x3r, gsend, grecv,
):
    NC = R * C // 2
    H = NC // 2
    RC = R // C
    Bl, dl = feat.shape
    hb = Bl // 2
    dr = protos.shape[0]
    kl = protos.shape[1] // R
    ratio = float(Bl * R) / float(protos.shape[1] * C)

    r = lax.axis_index("rows")
    c = lax.axis_index("cls")
    x, core = c // 2, c % 2

    def pos(r_, x_):
        p = snake(r_)
        return x_ * R + jnp.where(x_ % 2 == 0, p, R - 1 - p)

    def place(q_):
        x_ = q_ // R
        p = q_ % R
        return snake(jnp.where(x_ % 2 == 0, p, R - 1 - p)), x_

    q = pos(r, x)
    rr, rx = place((q + 1) % NC)
    lr, lx = place((q + NC - 1) % NC)
    right = (rr, rx * 2 + core)
    left = (lr, lx * 2 + core)
    partner = (r, x * 2 + 1 - core)

    def rpeer(o):
        return (r + o) % R

    def cpeer(o):
        return (c + o) % C

    barrier = pltpu.get_barrier_semaphore()

    def sig_r(o, _):
        pl.semaphore_signal(barrier, inc=1, device_id=(rpeer(o), c), device_id_type=MESH)
        return 0

    def sig_c(o, _):
        pl.semaphore_signal(barrier, inc=1, device_id=(r, cpeer(o)), device_id_type=MESH)
        return 0

    own = pltpu.make_async_copy(feat, G.at[q, core], lsem.at[0])
    own.start()
    lax.fori_loop(1, R, sig_r, 0)
    lax.fori_loop(1, C, sig_c, 0)
    pl.semaphore_wait(barrier, R + C - 2)
    own.wait()

    def half(q_, co, h):
        return G.at[q_, co, pl.ds(h * hb, hb)]

    def ring(s, h, to_right):
        o = (q - s + NC) % NC if to_right else (q + s) % NC
        ss, rs = (rs_s, rs_r) if to_right else (ls_s, ls_r)
        return pltpu.make_async_remote_copy(
            src_ref=half(o, core, h), dst_ref=half(o, core, h), send_sem=ss.at[s, h], recv_sem=rs.at[s, h],
            device_id=right if to_right else left, device_id_type=MESH,
        )

    def pair(d, s, h):
        o = (q - s + NC) % NC if d == 0 else (q + s) % NC
        return pltpu.make_async_remote_copy(
            src_ref=half(o, core, h), dst_ref=half(o, core, h), send_sem=psend.at[d, s, h], recv_sem=precv.at[d, s, h],
            device_id=partner, device_id_type=MESH,
        )

    def pair_in(d, s, h):
        o = (q - s + NC) % NC if d == 0 else (q + s) % NC
        return pltpu.make_async_remote_copy(
            src_ref=half(o, 1 - core, h), dst_ref=half(o, 1 - core, h), send_sem=psend.at[d, s, h], recv_sem=precv.at[d, s, h],
            device_id=partner, device_id_type=MESH,
        )

    for h in (0, 1):
        ring(0, h, True).start()
        ring(0, h, False).start()

    def proto_copy(o, slot_r):
        return pltpu.make_async_remote_copy(
            src_ref=protos.at[:, pl.ds(pl.multiple_of(rpeer(o) * kl, kl), kl)],
            dst_ref=Pb.at[slot_r // RC, pl.ds(pl.multiple_of((slot_r % RC) * dr, dr), dr)],
            send_sem=c_s.at[o], recv_sem=c_r.at[o],
            device_id=(rpeer(o), c), device_id_type=MESH,
        )

    def proto_start(o, _):
        proto_copy(o, r).start()
        return 0

    lax.fori_loop(1, R, proto_start, 0)
    mine = pltpu.make_async_copy(
        protos.at[:, pl.ds(pl.multiple_of(r * kl, kl), kl)],
        Pb.at[r // RC, pl.ds(pl.multiple_of((r % RC) * dr, dr), dr)],
        lsem.at[1],
    )
    mine.start()
    for h in (0, 1):
        pair(0, 0, h).start()

    def zero(i, _):
        S[i] = jnp.zeros(S.shape[1:], F32)
        return 0

    lax.fori_loop(0, R, zero, 0)

    def proto_wait(o, _):
        proto_copy(o, (r - o + R) % R).wait()
        return 0

    lax.fori_loop(1, R, proto_wait, 0)
    mine.wait()

    def turn(i, _):
        PT[i] = Pb[i].astype(F32).T.astype(BF16)
        return 0

    lax.fori_loop(0, C, turn, 0)

    def load(q_, co, slot):
        return pltpu.make_async_copy(G.at[q_, co], fbuf.at[slot], lsem.at[2 + slot])

    def absorb(blocks):
        for i, (q_, co) in enumerate(blocks):
            load(q_, co, i).start()
        for i, (q_, co) in enumerate(blocks):
            load(q_, co, i).wait()
            r_, x_ = place(q_)
            S[r_] += lax.dot_general(
                PT[x_ * 2 + co], fbuf[i], (((1,), (1,)), ((), ())), preferred_element_type=F32
            )

    def behind(s):
        return (q - s + NC) % NC

    def ahead(s):
        return (q + s) % NC

    def ring_step(s, _):
        for h in (0, 1):
            ring(s - 1, h, True).wait_recv()
            ring(s - 1, h, False).wait_recv()

            @pl.when(jnp.logical_or(s < H - 1, h == 0))
            def _():
                ring(s, h, True).start()

            @pl.when(jnp.logical_or(s < H - 1, h == 1))
            def _():
                ring(s, h, False).start()

            pair(0, s, h).start()
            pair(1, s, h).start()
            if h == 0:

                @pl.when(s == 1)
                def _():
                    for hh in (0, 1):
                        pair_in(0, 0, hh).wait_recv()
                    absorb([(q, core), (q, 1 - core)])

                @pl.when(s > 1)
                def _():
                    for hh in (0, 1):
                        pair_in(0, s - 1, hh).wait_recv()
                        pair_in(1, s - 1, hh).wait_recv()
                    absorb([(behind(s - 1), core), (ahead(s - 1), core), (behind(s - 1), 1 - core), (ahead(s - 1), 1 - core)])
        return 0

    lax.fori_loop(1, H, ring_step, 0)
    for hh in (0, 1):
        pair_in(0, H - 1, hh).wait_recv()
        pair_in(1, H - 1, hh).wait_recv()
    absorb(
        [(behind(H - 1), core), (ahead(H - 1), core), (behind(H - 1), 1 - core), (ahead(H - 1), 1 - core)]
    )
    ring(H - 1, 0, True).wait_recv()
    pair(0, H, 0).start()
    ring(H - 1, 1, False).wait_recv()
    pair(1, H, 1).start()
    pair_in(0, H, 0).wait_recv()
    pair_in(1, H, 1).wait_recv()
    absorb([(behind(H), core), (behind(H), 1 - core)])

    def exchange(e, st, s1, s2, qv, res, join):
        def one(o):
            return pltpu.make_async_remote_copy(
                src_ref=st.at[pl.ds(cpeer(o) * RC, RC)], dst_ref=s1.at[c],
                send_sem=x1s.at[e, o], recv_sem=x1r.at[e, o], device_id=(r, cpeer(o)), device_id_type=MESH,
            )

        for o in range(1, C):
            one(o).start()
        s1[c] = st[pl.ds(c * RC, RC)]
        for o in range(1, C):
            one(o).wait()
        qv[...] = join([s1[i] for i in range(C)])

        def two(o):
            return pltpu.make_async_remote_copy(
                src_ref=qv, dst_ref=s2.at[r],
                send_sem=x2s.at[e, o], recv_sem=x2r.at[e, o], device_id=(rpeer(o), c), device_id_type=MESH,
            )

        for o in range(1, R):
            two(o).start()
        s2[r] = qv[...]
        for o in range(1, R):
            two(o).wait()
        res[pl.ds(c * RC, RC)] = join([s2[i] for i in range(R)])

        def three(o):
            return pltpu.make_async_remote_copy(
                src_ref=res.at[pl.ds(c * RC, RC)], dst_ref=res.at[pl.ds(c * RC, RC)],
                send_sem=x3s.at[e, o], recv_sem=x3r.at[e, o], device_id=(r, cpeer(o)), device_id_type=MESH,
            )

        for o in range(1, C):
            three(o).start()
        for o in range(1, C):
            three(o).wait()

    def join_stats(parts):
        top = functools.reduce(jnp.maximum, [p[:, 0] for p in parts])
        s2 = sum(p[:, 1] * jnp.exp((p[:, 0] - top) / code_temp) for p in parts)
        s3 = sum(p[:, 2] * jnp.exp((p[:, 0] - top) / loss_temp) for p in parts)
        return jnp.stack([top, s2, s3], axis=1)

    def join_sum(parts):
        return functools.reduce(jnp.add, parts)

    def first(i, _):
        sc = S[i]
        top = jnp.max(sc, axis=0, keepdims=True)
        sh = sc - top
        e2 = jnp.exp(sh / code_temp)
        e3 = jnp.exp(sh / loss_temp)
        E[i] = e2
        S[i] = e3
        st0[i, 0] = top
        st0[i, 1] = jnp.sum(e2, axis=0, keepdims=True)
        st0[i, 2] = jnp.sum(e3, axis=0, keepdims=True)
        return 0

    lax.fori_loop(0, R, first, 0)
    exchange(0, st0, a1, a2, q0, res0, join_stats)

    def scales(i, _):
        down = st0[i, 0] - res0[i, 0]
        f2 = jnp.exp(down / code_temp)
        fv[i] = f2
        wv[i] = f2 / res0[i, 1]
        av[i] = jnp.exp(down / loss_temp) / res0[i, 2]
        return 0

    lax.fori_loop(0, R, scales, 0)

    for sweep in range(ITERS):

        def col(i, acc):
            m = E[i] * wv[i]
            return acc + functools.reduce(jnp.add, [m[:, j * 128 : (j + 1) * 128] for j in range(Bl // 128)])

        mass = lax.fori_loop(0, R, col, jnp.zeros((kl, 128), F32))
        cs[...] = jnp.broadcast_to(ratio / jnp.sum(mass, axis=1, keepdims=True), (kl, 128))

        def row(i, _):
            st1[sweep, i, 0] = jnp.sum(E[i] * cs[:, 0:1], axis=0, keepdims=True) * fv[i]
            return 0

        lax.fori_loop(0, R, row, 0)
        exchange(sweep + 1, st1.at[sweep], b1.at[sweep], b2.at[sweep], q1.at[sweep], res1.at[sweep], join_sum)

        def rescale(i, _):
            wv[i] = fv[i] / res1[sweep, i, 0]
            return 0

        lax.fori_loop(0, R, rescale, 0)

    def slope(i, _):
        SL[i] = ((S[i] * av[i] - E[i] * wv[i] * cs[:, 0:1]) / loss_temp).astype(BF16)
        return 0

    lax.fori_loop(0, R, slope, 0)

    def block_of(t):
        return (t + 1 + r // RC) % C

    def grad_load(n):
        cb = block_of(n // R)
        return load(pos(n % R, cb // 2), cb % 2, n % 2)

    def grad_copy(t, j, src_r):
        dest = block_of(t) * RC + j
        return pltpu.make_async_remote_copy(
            src_ref=sendb.at[t, pl.ds(pl.multiple_of(j * dr, dr), dr)],
            dst_ref=out.at[:, pl.ds(pl.multiple_of(src_r * kl, kl), kl)],
            send_sem=gsend.at[t, j], recv_sem=grecv.at[src_r],
            device_id=(dest, c), device_id_type=MESH,
        )

    def own_grad():
        return pltpu.make_async_copy(
            sendb.at[C - 1, pl.ds(pl.multiple_of((r % RC) * dr, dr), dr)],
            out.at[:, pl.ds(pl.multiple_of(r * kl, kl), kl)],
            lsem.at[1],
        )

    grad_load(0).start()

    def grad(n, _):
        t = n // R

        @pl.when(n + 1 < R * C)
        def _():
            grad_load(n + 1).start()

        grad_load(n).wait()
        part = jnp.dot(SL[n % R], fbuf[n % 2], preferred_element_type=F32)

        @pl.when(n % R == 0)
        def _():
            GT[...] = part

        @pl.when(n % R > 0)
        def _():
            GT[...] += part

        @pl.when(n % R == R - 1)
        def _():
            sendb[t] = GT[...].T.astype(BF16)
            for j in range(RC):

                @pl.when(block_of(t) * RC + j != r)
                def _():
                    grad_copy(t, j, r).start()

                @pl.when(block_of(t) * RC + j == r)
                def _():
                    own_grad().start()

        return 0

    lax.fori_loop(0, R * C, grad, 0)

    def drain(s, _):
        for h in (0, 1):

            @pl.when(jnp.logical_or(s < H - 1, h == 0))
            def _():
                ring(s, h, True).wait_send()

            @pl.when(jnp.logical_or(s < H - 1, h == 1))
            def _():
                ring(s, h, False).wait_send()

            pair(0, s, h).wait_send()

            @pl.when(s > 0)
            def _():
                pair(1, s, h).wait_send()

        return 0

    lax.fori_loop(0, H, drain, 0)
    pair(0, H, 0).wait_send()
    pair(1, H, 1).wait_send()
    own_grad().wait()

    def sent(n, _):
        @pl.when(block_of(n // RC) * RC + n % RC != r)
        def _():
            grad_copy(n // RC, n % RC, r).wait_send()

        return 0

    lax.fori_loop(0, C * RC, sent, 0)

    def got(o, _):
        grad_copy(0, 0, rpeer(o)).wait_recv()
        return 0

    lax.fori_loop(1, R, got, 0)


def solution(mesh):
    R, C = mesh.shape["rows"], mesh.shape["cls"]

    def local(features, prototypes):
        Bl, dl = features.shape
        dr, kc = prototypes.shape
        kl = kc // R
        NC, RC = R * C // 2, R // C
        H = NC // 2
        X = ITERS + 1
        dma = pltpu.SemaphoreType.DMA
        V = pltpu.VMEM
        out, _ = pl.pallas_call(
            functools.partial(kernel, R, C),
            out_shape=(
                jax.ShapeDtypeStruct((dr, kc), BF16),
                jax.ShapeDtypeStruct((NC, 2, Bl, dl), BF16),
            ),
            in_specs=[pl.BlockSpec(memory_space=pl.ANY)] * 2,
            out_specs=(pl.BlockSpec(memory_space=pl.ANY),) * 2,
            scratch_shapes=[
                V((C, dl, kl), BF16),
                V((C, kl, dl), BF16),
                V((R, kl, Bl), F32),
                V((R, kl, Bl), F32),
                V((R, kl, Bl), BF16),
                V((kl, dl), F32),
                V((4, Bl, dl), BF16),
                V((C, dl, kl), BF16),
                V((R, 3, 1, Bl), F32),
                V((ITERS, R, 1, 1, Bl), F32),
                V((C, RC, 3, 1, Bl), F32),
                V((R, RC, 3, 1, Bl), F32),
                V((ITERS, C, RC, 1, 1, Bl), F32),
                V((ITERS, R, RC, 1, 1, Bl), F32),
                V((RC, 3, 1, Bl), F32),
                V((ITERS, RC, 1, 1, Bl), F32),
                V((R, 3, 1, Bl), F32),
                V((ITERS, R, 1, 1, Bl), F32),
                V((R, 1, Bl), F32),
                V((R, 1, Bl), F32),
                V((R, 1, Bl), F32),
                V((kl, 128), F32),
                dma((6,)),
                dma((2, H + 1, 2)),
                dma((2, H + 1, 2)),
                dma((H, 2)),
                dma((H, 2)),
                dma((H, 2)),
                dma((H, 2)),
                dma((R,)),
                dma((R,)),
                dma((X, C)),
                dma((X, C)),
                dma((X, R)),
                dma((X, R)),
                dma((X, C)),
                dma((X, C)),
                dma((C, RC)),
                dma((R,)),
            ],
            compiler_params=pltpu.CompilerParams(
                collective_id=0, has_side_effects=True, vmem_limit_bytes=60 * 1024 * 1024
            ),
        )(features, prototypes)
        return out.astype(F32)

    return jax.shard_map(
        local,
        mesh=mesh,
        in_specs=(P("rows", "cls"), P("rows", "cls")),
        out_specs=P("rows", "cls"),
        check_vma=False,
    )
```

```python
import functools

import jax
import jax.numpy as jnp
from jax import lax
from jax.experimental import pallas as pl
from jax.experimental.pallas import tpu as pltpu
from jax.sharding import PartitionSpec as P

ITERS = 3
code_temp = 0.2
loss_temp = 0.3

MESH = pl.DeviceIdType.MESH
F32 = jnp.float32
BF16 = jnp.bfloat16


def kernel(
    R, C, feat, protos, out, G, Pb, PT, S, E, SL, GT, fbuf, sendb, st0, st1, a1, a2, b1, b2, q0, q1, res0, res1, wv, av, fv, cs,
    lsem, ps, pr, up_s, dn_s, ln_r, ns, nr, ds_, dr_, c_s, c_r, x1s, x1r, x2s, x2r, x3s, x3r, gsend, grecv,
):
    Z = R // 2
    RC = R // C
    Bl, dl = feat.shape
    hb = Bl // 2
    dr = protos.shape[0]
    kl = protos.shape[1] // R
    ratio = float(Bl * R) / float(protos.shape[1] * C)

    r = lax.axis_index("rows")
    c = lax.axis_index("cls")
    x, core = c // 2, c % 2
    z, y = r // 2, r % 2
    x_near = (r, (1 - x) * 2 + core)
    y_near = (2 * z + 1 - y, c)
    partner = (r, x * 2 + 1 - core)

    def rpeer(o):
        return (r + o) % R

    def cpeer(o):
        return (c + o) % C

    barrier = pltpu.get_barrier_semaphore()

    def sig_r(o, _):
        pl.semaphore_signal(barrier, inc=1, device_id=(rpeer(o), c), device_id_type=MESH)
        return 0

    def sig_c(o, _):
        pl.semaphore_signal(barrier, inc=1, device_id=(r, cpeer(o)), device_id_type=MESH)
        return 0

    own = pltpu.make_async_copy(feat, G.at[r, c], lsem.at[0])
    own.start()
    lax.fori_loop(1, R, sig_r, 0)
    lax.fori_loop(1, C, sig_c, 0)
    pl.semaphore_wait(barrier, R + C - 2)
    own.wait()

    def half(quad, o, h, co):
        xq = 1 - x if quad in (1, 3) else x
        yq = 1 - y if quad in (2, 3) else y
        return G.at[2 * o + yq, 2 * xq + co, pl.ds(h * hb, hb)]

    def send(src, send_sem, recv_sem, dest):
        return pltpu.make_async_remote_copy(
            src_ref=src, dst_ref=src, send_sem=send_sem, recv_sem=recv_sem, device_id=dest, device_id_type=MESH
        )

    def line_up(o, h):
        return send(half(0, o, h, core), up_s.at[o, h], ln_r.at[o, h], (r + 2, c))

    def line_down(o, h):
        return send(half(0, o, h, core), dn_s.at[o, h], ln_r.at[o, h], (r - 2, c))

    def line_in(o, h):
        return send(half(0, o, h, core), up_s.at[o, h], ln_r.at[o, h], partner)

    def near(axis, o, h):
        return send(half(0, o, h, core), ns.at[axis, o, h], nr.at[axis, o, h], (x_near, y_near)[axis])

    def near_in(axis, o, h):
        return send(half(1 + axis, o, h, core), ns.at[axis, o, h], nr.at[axis, o, h], (x_near, y_near)[axis])

    def diag(h, o):
        return send(half(2 - h, o, h, core), ds_.at[o, h], dr_.at[o, h], (x_near, y_near)[h])

    def diag_in(h, o):
        return send(half(3, o, h, core), ds_.at[o, h], dr_.at[o, h], (x_near, y_near)[h])

    def pair(quad, o, h):
        return send(half(quad, o, h, core), ps.at[quad, o, h], pr.at[quad, o, h], partner)

    def pair_in(quad, o, h):
        return send(half(quad, o, h, 1 - core), ps.at[quad, o, h], pr.at[quad, o, h], partner)

    def sides(k, fn):
        if isinstance(k, int) and k == 0:
            fn(z, None)
            return

        @pl.when(z - k >= 0)
        def _():
            fn(z - k, 0)

        @pl.when(z + k < Z)
        def _():
            fn(z + k, 1)

    def do_line(k):
        def step(o, side):
            for h in (0, 1):
                if side is not None:
                    line_in(o, h).wait_recv()
                if side != 1:

                    @pl.when(z + 1 < Z)
                    def _():
                        line_up(o, h).start()

                if side != 0:

                    @pl.when(z >= 1)
                    def _():
                        line_down(o, h).start()

                near(0, o, h).start()
                near(1, o, h).start()
                pair(0, o, h).start()

        sides(k, step)

    def do_near(k):
        def step(o, side):
            for h in (0, 1):
                for axis in (1, 0):
                    near_in(axis, o, h).wait_recv()
                    if axis == 1 - h:
                        diag(h, o).start()
                    pair(1 + axis, o, h).start()

        sides(k, step)

    def do_diag(k):
        def step(o, side):
            for h in (0, 1):
                diag_in(h, o).wait_recv()
                pair(3, o, h).start()

        sides(k, step)

    do_line(0)

    def proto_copy(o, slot_r):
        return pltpu.make_async_remote_copy(
            src_ref=protos.at[:, pl.ds(pl.multiple_of(rpeer(o) * kl, kl), kl)],
            dst_ref=Pb.at[slot_r // RC, pl.ds(pl.multiple_of((slot_r % RC) * dr, dr), dr)],
            send_sem=c_s.at[o], recv_sem=c_r.at[o],
            device_id=(rpeer(o), c), device_id_type=MESH,
        )

    def proto_start(o, _):
        proto_copy(o, r).start()
        return 0

    lax.fori_loop(1, R, proto_start, 0)
    mine = pltpu.make_async_copy(
        protos.at[:, pl.ds(pl.multiple_of(r * kl, kl), kl)],
        Pb.at[r // RC, pl.ds(pl.multiple_of((r % RC) * dr, dr), dr)],
        lsem.at[1],
    )
    mine.start()
    def zero(i, _):
        S[i] = jnp.zeros(S.shape[1:], F32)
        return 0

    lax.fori_loop(0, R, zero, 0)

    def proto_wait(o, _):
        proto_copy(o, (r - o + R) % R).wait()
        return 0

    lax.fori_loop(1, R, proto_wait, 0)
    mine.wait()

    def turn(i, _):
        PT[i] = Pb[i].astype(F32).T.astype(BF16)
        return 0

    lax.fori_loop(0, C, turn, 0)

    def load(r_, c_, slot):
        return pltpu.make_async_copy(G.at[r_, c_], fbuf.at[slot], lsem.at[2 + slot])

    def absorb(quads, k):
        def step(o, side):
            blocks = []
            for quad in quads:
                for h in (0, 1):
                    pair_in(quad, o, h).wait_recv()
                xq = 1 - x if quad in (1, 3) else x
                yq = 1 - y if quad in (2, 3) else y
                blocks += [(2 * o + yq, 2 * xq + core), (2 * o + yq, 2 * xq + 1 - core)]
            for i, (r_, c_) in enumerate(blocks):
                load(r_, c_, i).start()
            for i, (r_, c_) in enumerate(blocks):
                load(r_, c_, i).wait()
                S[r_] += lax.dot_general(PT[c_], fbuf[i], (((1,), (1,)), ((), ())), preferred_element_type=F32)

        sides(k, step)

    do_line(1)
    do_near(0)
    absorb((0,), 0)

    def later(k, _):
        @pl.when(k < Z)
        def _():
            do_line(k)

        do_near(k - 1)
        absorb((0,), k - 1)

        @pl.when(k == 2)
        def _():
            do_diag(0)
            absorb((1, 2), 0)
            absorb((3,), 0)

        @pl.when(k > 2)
        def _():
            do_diag(k - 2)
            absorb((1, 2), k - 2)
            absorb((3,), k - 2)

        return 0

    lax.fori_loop(2, Z + 1, later, 0)
    absorb((1, 2), Z - 1)
    do_diag(Z - 1)
    absorb((3,), Z - 1)

    def exchange(e, st, s1, s2, qv, res, join):
        def one(o):
            return pltpu.make_async_remote_copy(
                src_ref=st.at[pl.ds(cpeer(o) * RC, RC)], dst_ref=s1.at[c],
                send_sem=x1s.at[e, o], recv_sem=x1r.at[e, o], device_id=(r, cpeer(o)), device_id_type=MESH,
            )

        for o in range(1, C):
            one(o).start()
        s1[c] = st[pl.ds(c * RC, RC)]
        for o in range(1, C):
            one(o).wait()
        qv[...] = join([s1[i] for i in range(C)])

        def two(o):
            return pltpu.make_async_remote_copy(
                src_ref=qv, dst_ref=s2.at[r],
                send_sem=x2s.at[e, o], recv_sem=x2r.at[e, o], device_id=(rpeer(o), c), device_id_type=MESH,
            )

        for o in range(1, R):
            two(o).start()
        s2[r] = qv[...]
        for o in range(1, R):
            two(o).wait()
        res[pl.ds(c * RC, RC)] = join([s2[i] for i in range(R)])

        def three(o):
            return pltpu.make_async_remote_copy(
                src_ref=res.at[pl.ds(c * RC, RC)], dst_ref=res.at[pl.ds(c * RC, RC)],
                send_sem=x3s.at[e, o], recv_sem=x3r.at[e, o], device_id=(r, cpeer(o)), device_id_type=MESH,
            )

        for o in range(1, C):
            three(o).start()
        for o in range(1, C):
            three(o).wait()

    def join_stats(parts):
        top = functools.reduce(jnp.maximum, [p[:, 0] for p in parts])
        s2 = sum(p[:, 1] * jnp.exp((p[:, 0] - top) / code_temp) for p in parts)
        s3 = sum(p[:, 2] * jnp.exp((p[:, 0] - top) / loss_temp) for p in parts)
        return jnp.stack([top, s2, s3], axis=1)

    def join_sum(parts):
        return functools.reduce(jnp.add, parts)

    def first(i, _):
        sc = S[i]
        top = jnp.max(sc, axis=0, keepdims=True)
        sh = sc - top
        e2 = jnp.exp(sh / code_temp)
        e3 = jnp.exp(sh / loss_temp)
        E[i] = e2
        S[i] = e3
        st0[i, 0] = top
        st0[i, 1] = jnp.sum(e2, axis=0, keepdims=True)
        st0[i, 2] = jnp.sum(e3, axis=0, keepdims=True)
        return 0

    lax.fori_loop(0, R, first, 0)
    exchange(0, st0, a1, a2, q0, res0, join_stats)

    def scales(i, _):
        down = st0[i, 0] - res0[i, 0]
        f2 = jnp.exp(down / code_temp)
        fv[i] = f2
        wv[i] = f2 / res0[i, 1]
        av[i] = jnp.exp(down / loss_temp) / res0[i, 2]
        return 0

    lax.fori_loop(0, R, scales, 0)

    for sweep in range(ITERS):

        def col(i, acc):
            m = E[i] * wv[i]
            return acc + functools.reduce(jnp.add, [m[:, j * 128 : (j + 1) * 128] for j in range(Bl // 128)])

        mass = lax.fori_loop(0, R, col, jnp.zeros((kl, 128), F32))
        cs[...] = jnp.broadcast_to(ratio / jnp.sum(mass, axis=1, keepdims=True), (kl, 128))

        def row(i, _):
            st1[sweep, i, 0] = jnp.sum(E[i] * cs[:, 0:1], axis=0, keepdims=True) * fv[i]
            return 0

        lax.fori_loop(0, R, row, 0)
        exchange(sweep + 1, st1.at[sweep], b1.at[sweep], b2.at[sweep], q1.at[sweep], res1.at[sweep], join_sum)

        def rescale(i, _):
            wv[i] = fv[i] / res1[sweep, i, 0]
            return 0

        lax.fori_loop(0, R, rescale, 0)

    def slope(i, _):
        SL[i] = ((S[i] * av[i] - E[i] * wv[i] * cs[:, 0:1]) / loss_temp).astype(BF16)
        return 0

    lax.fori_loop(0, R, slope, 0)

    def block_of(t):
        g = r // RC
        return (2 * (g // 2) + 2 * (1 - t // 2)) % 4 + (g + 1 - t % 2) % 2

    def grad_load(n):
        cb = block_of(n // R)
        return load(n % R, cb, n % 2)

    def grad_copy(t, j, src_r):
        dest = block_of(t) * RC + j
        return pltpu.make_async_remote_copy(
            src_ref=sendb.at[t, pl.ds(pl.multiple_of(j * dr, dr), dr)],
            dst_ref=out.at[:, pl.ds(pl.multiple_of(src_r * kl, kl), kl)],
            send_sem=gsend.at[t, j], recv_sem=grecv.at[src_r],
            device_id=(dest, c), device_id_type=MESH,
        )

    def own_grad():
        return pltpu.make_async_copy(
            sendb.at[C - 1, pl.ds(pl.multiple_of((r % RC) * dr, dr), dr)],
            out.at[:, pl.ds(pl.multiple_of(r * kl, kl), kl)],
            lsem.at[1],
        )

    grad_load(0).start()

    def grad(n, _):
        t = n // R

        @pl.when(n + 1 < R * C)
        def _():
            grad_load(n + 1).start()

        grad_load(n).wait()
        part = jnp.dot(SL[n % R], fbuf[n % 2], preferred_element_type=F32)

        @pl.when(n % R == 0)
        def _():
            GT[...] = part

        @pl.when(n % R > 0)
        def _():
            GT[...] += part

        @pl.when(n % R == R - 1)
        def _():
            sendb[t] = GT[...].T.astype(BF16)
            for j in range(RC):

                @pl.when(block_of(t) * RC + j != r)
                def _():
                    grad_copy(t, j, r).start()

                @pl.when(block_of(t) * RC + j == r)
                def _():
                    own_grad().start()

        return 0

    lax.fori_loop(0, R * C, grad, 0)

    def drain(o, _):
        for h in (0, 1):

            @pl.when(jnp.logical_and(o <= z, z + 1 < Z))
            def _():
                line_up(o, h).wait_send()

            @pl.when(jnp.logical_and(o >= z, z >= 1))
            def _():
                line_down(o, h).wait_send()

            near(0, o, h).wait_send()
            near(1, o, h).wait_send()
            diag(h, o).wait_send()
            for quad in range(4):
                pair(quad, o, h).wait_send()

        return 0

    lax.fori_loop(0, Z, drain, 0)
    own_grad().wait()

    def sent(n, _):
        @pl.when(block_of(n // RC) * RC + n % RC != r)
        def _():
            grad_copy(n // RC, n % RC, r).wait_send()

        return 0

    lax.fori_loop(0, C * RC, sent, 0)

    def got(o, _):
        grad_copy(0, 0, rpeer(o)).wait_recv()
        return 0

    lax.fori_loop(1, R, got, 0)


def solution(mesh):
    R, C = mesh.shape["rows"], mesh.shape["cls"]
    assert C == 4 and R % 4 == 0

    def local(features, prototypes):
        Bl, dl = features.shape
        dr, kc = prototypes.shape
        kl = kc // R
        Z, RC = R // 2, R // C
        X = ITERS + 1
        dma = pltpu.SemaphoreType.DMA
        V = pltpu.VMEM
        out, _ = pl.pallas_call(
            functools.partial(kernel, R, C),
            out_shape=(
                jax.ShapeDtypeStruct((dr, kc), BF16),
                jax.ShapeDtypeStruct((R, C, Bl, dl), BF16),
            ),
            in_specs=[pl.BlockSpec(memory_space=pl.ANY)] * 2,
            out_specs=(pl.BlockSpec(memory_space=pl.ANY),) * 2,
            scratch_shapes=[
                V((C, dl, kl), BF16),
                V((C, kl, dl), BF16),
                V((R, kl, Bl), F32),
                V((R, kl, Bl), F32),
                V((R, kl, Bl), BF16),
                V((kl, dl), F32),
                V((4, Bl, dl), BF16),
                V((C, dl, kl), BF16),
                V((R, 3, 1, Bl), F32),
                V((ITERS, R, 1, 1, Bl), F32),
                V((C, RC, 3, 1, Bl), F32),
                V((R, RC, 3, 1, Bl), F32),
                V((ITERS, C, RC, 1, 1, Bl), F32),
                V((ITERS, R, RC, 1, 1, Bl), F32),
                V((RC, 3, 1, Bl), F32),
                V((ITERS, RC, 1, 1, Bl), F32),
                V((R, 3, 1, Bl), F32),
                V((ITERS, R, 1, 1, Bl), F32),
                V((R, 1, Bl), F32),
                V((R, 1, Bl), F32),
                V((R, 1, Bl), F32),
                V((kl, 128), F32),
                dma((6,)),
                dma((4, Z, 2)),
                dma((4, Z, 2)),
                dma((Z, 2)),
                dma((Z, 2)),
                dma((Z, 2)),
                dma((2, Z, 2)),
                dma((2, Z, 2)),
                dma((Z, 2)),
                dma((Z, 2)),
                dma((R,)),
                dma((R,)),
                dma((X, C)),
                dma((X, C)),
                dma((X, R)),
                dma((X, R)),
                dma((X, C)),
                dma((X, C)),
                dma((C, RC)),
                dma((R,)),
            ],
            compiler_params=pltpu.CompilerParams(
                collective_id=0, has_side_effects=True, vmem_limit_bytes=60 * 1024 * 1024
            ),
        )(features, prototypes)
        return out.astype(F32)

    return jax.shard_map(
        local,
        mesh=mesh,
        in_specs=(P("rows", "cls"), P("rows", "cls")),
        out_specs=P("rows", "cls"),
        check_vma=False,
    )
```

```python
import functools

import jax
import jax.numpy as jnp
from jax import lax
from jax.experimental import pallas as pl
from jax.experimental.pallas import tpu as pltpu
from jax.sharding import PartitionSpec as P

ITERS = 3
code_temp = 0.2
loss_temp = 0.3

MESH = pl.DeviceIdType.MESH
F32 = jnp.float32
BF16 = jnp.bfloat16


def kernel(
    R, C, feat, protos, out, G, Pb, PT, S, E, SL, GT, fbuf, sendb, st0, st1, a1, a2, b1, b2, q0, q1, res0, res1, wv, av, fv, cs,
    lsem, ps, pr, up_s, dn_s, ln_r, ns, nr, ds_, dr_, c_s, c_r, x1s, x1r, x2s, x2r, x3s, x3r, gsend, grecv,
):
    Z = R // 2
    RC = R // C
    Bl, dl = feat.shape
    hb = Bl // 2
    dr = protos.shape[0]
    kl = protos.shape[1] // R
    ratio = float(Bl * R) / float(protos.shape[1] * C)

    r = lax.axis_index("rows")
    c = lax.axis_index("cls")
    x, core = c // 2, c % 2
    z, y = r // 2, r % 2
    x_near = (r, (1 - x) * 2 + core)
    y_near = (2 * z + 1 - y, c)
    partner = (r, x * 2 + 1 - core)

    def rpeer(o):
        return (r + o) % R

    def cpeer(o):
        return (c + o) % C

    barrier = pltpu.get_barrier_semaphore()

    def sig_r(o, _):
        pl.semaphore_signal(barrier, inc=1, device_id=(rpeer(o), c), device_id_type=MESH)
        return 0

    def sig_c(o, _):
        pl.semaphore_signal(barrier, inc=1, device_id=(r, cpeer(o)), device_id_type=MESH)
        return 0

    own = pltpu.make_async_copy(feat, G.at[r, c], lsem.at[0])
    own.start()
    lax.fori_loop(1, R, sig_r, 0)
    lax.fori_loop(1, C, sig_c, 0)
    pl.semaphore_wait(barrier, R + C - 2)

    def half(quad, o, h, co):
        xq = 1 - x if quad in (1, 3) else x
        yq = 1 - y if quad in (2, 3) else y
        return G.at[2 * o + yq, 2 * xq + co, pl.ds(h * hb, hb)]

    def send(dst, send_sem, recv_sem, dest, src=None):
        return pltpu.make_async_remote_copy(
            src_ref=dst if src is None else src, dst_ref=dst, send_sem=send_sem, recv_sem=recv_sem, device_id=dest, device_id_type=MESH
        )

    def line_up(o, h, src=None):
        return send(half(0, o, h, core), up_s.at[o, h], ln_r.at[o, h], (r + 2, c), src)

    def line_down(o, h, src=None):
        return send(half(0, o, h, core), dn_s.at[o, h], ln_r.at[o, h], (r - 2, c), src)

    def line_in(o, h):
        return send(half(0, o, h, core), up_s.at[o, h], ln_r.at[o, h], partner)

    def near(axis, o, h, src=None):
        return send(half(0, o, h, core), ns.at[axis, o, h], nr.at[axis, o, h], (x_near, y_near)[axis], src)

    def near_in(axis, o, h):
        return send(half(1 + axis, o, h, core), ns.at[axis, o, h], nr.at[axis, o, h], (x_near, y_near)[axis])

    def diag(h, o):
        return send(half(2 - h, o, h, core), ds_.at[o, h], dr_.at[o, h], (x_near, y_near)[h])

    def diag_in(h, o):
        return send(half(3, o, h, core), ds_.at[o, h], dr_.at[o, h], (x_near, y_near)[h])

    def pair(quad, o, h, src=None):
        return send(half(quad, o, h, core), ps.at[quad, o, h], pr.at[quad, o, h], partner, src)

    def pair_in(quad, o, h):
        return send(half(quad, o, h, 1 - core), ps.at[quad, o, h], pr.at[quad, o, h], partner)

    def sides(k, fn):
        if isinstance(k, int) and k == 0:
            fn(z, None)
            return

        @pl.when(z - k >= 0)
        def _():
            fn(z - k, 0)

        @pl.when(z + k < Z)
        def _():
            fn(z + k, 1)

    def do_line(k):
        def step(o, side):
            for h in (0, 1):
                src = feat.at[pl.ds(h * hb, hb)] if side is None else None
                if side is not None:
                    line_in(o, h).wait_recv()
                if side != 1:

                    @pl.when(z + 1 < Z)
                    def _():
                        line_up(o, h, src).start()

                if side != 0:

                    @pl.when(z >= 1)
                    def _():
                        line_down(o, h, src).start()

                near(0, o, h, src).start()
                near(1, o, h, src).start()
                pair(0, o, h, src).start()

        sides(k, step)

    def do_near(k):
        def step(o, side):
            for h in (0, 1):
                for axis in (1, 0):
                    near_in(axis, o, h).wait_recv()
                    if axis == 1 - h:
                        diag(h, o).start()
                    pair(1 + axis, o, h).start()

        sides(k, step)

    def do_diag(k):
        def step(o, side):
            for h in (0, 1):
                diag_in(h, o).wait_recv()
                pair(3, o, h).start()

        sides(k, step)

    do_line(0)

    def proto_copy(o, slot_r):
        return pltpu.make_async_remote_copy(
            src_ref=protos.at[:, pl.ds(pl.multiple_of(rpeer(o) * kl, kl), kl)],
            dst_ref=Pb.at[slot_r // RC, pl.ds(pl.multiple_of((slot_r % RC) * dr, dr), dr)],
            send_sem=c_s.at[o], recv_sem=c_r.at[o],
            device_id=(rpeer(o), c), device_id_type=MESH,
        )

    def proto_start(o, _):
        proto_copy(o, r).start()
        return 0

    lax.fori_loop(1, R, proto_start, 0)
    mine = pltpu.make_async_copy(
        protos.at[:, pl.ds(pl.multiple_of(r * kl, kl), kl)],
        Pb.at[r // RC, pl.ds(pl.multiple_of((r % RC) * dr, dr), dr)],
        lsem.at[1],
    )
    mine.start()
    def zero(i, _):
        S[i] = jnp.zeros(S.shape[1:], F32)
        return 0

    lax.fori_loop(0, R, zero, 0)

    def proto_wait(o, _):
        proto_copy(o, (r - o + R) % R).wait()
        return 0

    def turn(i, _):
        PT[i] = Pb[i].astype(F32).T.astype(BF16)
        return 0

    def prepare():
        lax.fori_loop(1, R, proto_wait, 0)
        mine.wait()
        lax.fori_loop(0, C, turn, 0)
        own.wait()

    def load(r_, c_, slot):
        return pltpu.make_async_copy(G.at[r_, c_], fbuf.at[slot], lsem.at[2 + slot])

    def absorb(quads, k):
        def step(o, side):
            blocks = []
            for quad in quads:
                for h in (0, 1):
                    pair_in(quad, o, h).wait_recv()
                xq = 1 - x if quad in (1, 3) else x
                yq = 1 - y if quad in (2, 3) else y
                blocks += [(2 * o + yq, 2 * xq + core), (2 * o + yq, 2 * xq + 1 - core)]
            for i, (r_, c_) in enumerate(blocks):
                load(r_, c_, i).start()
            for i, (r_, c_) in enumerate(blocks):
                load(r_, c_, i).wait()
                S[r_] += lax.dot_general(PT[c_], fbuf[i], (((1,), (1,)), ((), ())), preferred_element_type=F32)

        sides(k, step)

    do_line(1)
    do_near(0)

    def later(k, _):
        @pl.when(k < Z)
        def _():
            do_line(k)

        do_near(k - 1)

        @pl.when(k == 2)
        def _():
            do_diag(0)
            prepare()
            absorb((0,), 0)
            absorb((1, 2), 0)
            absorb((3,), 0)

        absorb((0,), k - 1)

        @pl.when(k > 2)
        def _():
            do_diag(k - 2)
            absorb((1, 2), k - 2)
            absorb((3,), k - 2)

        return 0

    lax.fori_loop(2, Z + 1, later, 0)
    absorb((1, 2), Z - 1)
    do_diag(Z - 1)
    absorb((3,), Z - 1)

    def exchange(e, st, s1, s2, qv, res, join):
        def one(o):
            return pltpu.make_async_remote_copy(
                src_ref=st.at[pl.ds(cpeer(o) * RC, RC)], dst_ref=s1.at[c],
                send_sem=x1s.at[e, o], recv_sem=x1r.at[e, o], device_id=(r, cpeer(o)), device_id_type=MESH,
            )

        for o in range(1, C):
            one(o).start()
        s1[c] = st[pl.ds(c * RC, RC)]
        for o in range(1, C):
            one(o).wait()
        qv[...] = join([s1[i] for i in range(C)])

        def two(o):
            return pltpu.make_async_remote_copy(
                src_ref=qv, dst_ref=s2.at[r],
                send_sem=x2s.at[e, o], recv_sem=x2r.at[e, o], device_id=(rpeer(o), c), device_id_type=MESH,
            )

        for o in range(1, R):
            two(o).start()
        s2[r] = qv[...]
        for o in range(1, R):
            two(o).wait()
        res[pl.ds(c * RC, RC)] = join([s2[i] for i in range(R)])

        def three(o):
            return pltpu.make_async_remote_copy(
                src_ref=res.at[pl.ds(c * RC, RC)], dst_ref=res.at[pl.ds(c * RC, RC)],
                send_sem=x3s.at[e, o], recv_sem=x3r.at[e, o], device_id=(r, cpeer(o)), device_id_type=MESH,
            )

        for o in range(1, C):
            three(o).start()
        for o in range(1, C):
            three(o).wait()

    def join_stats(parts):
        top = functools.reduce(jnp.maximum, [p[:, 0] for p in parts])
        s2 = sum(p[:, 1] * jnp.exp((p[:, 0] - top) / code_temp) for p in parts)
        s3 = sum(p[:, 2] * jnp.exp((p[:, 0] - top) / loss_temp) for p in parts)
        return jnp.stack([top, s2, s3], axis=1)

    def join_sum(parts):
        return functools.reduce(jnp.add, parts)

    def first(i, _):
        sc = S[i]
        top = jnp.max(sc, axis=0, keepdims=True)
        sh = sc - top
        e2 = jnp.exp(sh / code_temp)
        e3 = jnp.exp(sh / loss_temp)
        E[i] = e2
        S[i] = e3
        st0[i, 0] = top
        st0[i, 1] = jnp.sum(e2, axis=0, keepdims=True)
        st0[i, 2] = jnp.sum(e3, axis=0, keepdims=True)
        return 0

    lax.fori_loop(0, R, first, 0)
    exchange(0, st0, a1, a2, q0, res0, join_stats)

    def scales(i, _):
        down = st0[i, 0] - res0[i, 0]
        f2 = jnp.exp(down / code_temp)
        fv[i] = f2
        wv[i] = f2 / res0[i, 1]
        av[i] = jnp.exp(down / loss_temp) / res0[i, 2]
        return 0

    lax.fori_loop(0, R, scales, 0)

    for sweep in range(ITERS):

        def col(i, acc):
            m = E[i] * wv[i]
            return acc + functools.reduce(jnp.add, [m[:, j * 128 : (j + 1) * 128] for j in range(Bl // 128)])

        mass = lax.fori_loop(0, R, col, jnp.zeros((kl, 128), F32))
        cs[...] = jnp.broadcast_to(ratio / jnp.sum(mass, axis=1, keepdims=True), (kl, 128))

        def row(i, _):
            st1[sweep, i, 0] = jnp.sum(E[i] * cs[:, 0:1], axis=0, keepdims=True) * fv[i]
            return 0

        lax.fori_loop(0, R, row, 0)
        exchange(sweep + 1, st1.at[sweep], b1.at[sweep], b2.at[sweep], q1.at[sweep], res1.at[sweep], join_sum)

        def rescale(i, _):
            wv[i] = fv[i] / res1[sweep, i, 0]
            return 0

        lax.fori_loop(0, R, rescale, 0)

    def slope(i, _):
        SL[i] = ((S[i] * av[i] - E[i] * wv[i] * cs[:, 0:1]) / loss_temp).astype(BF16)
        return 0

    lax.fori_loop(0, R, slope, 0)

    def block_of(t):
        g = r // RC
        return (2 * (g // 2) + 2 * (1 - t // 2)) % 4 + (g + 1 - t % 2) % 2

    def grad_load(n):
        cb = block_of(n // R)
        return load(n % R, cb, n % 2)

    def grad_copy(t, j, src_r):
        dest = block_of(t) * RC + j
        return pltpu.make_async_remote_copy(
            src_ref=sendb.at[t, pl.ds(pl.multiple_of(j * dr, dr), dr)],
            dst_ref=out.at[:, pl.ds(pl.multiple_of(src_r * kl, kl), kl)],
            send_sem=gsend.at[t, j], recv_sem=grecv.at[src_r],
            device_id=(dest, c), device_id_type=MESH,
        )

    def own_grad():
        return pltpu.make_async_copy(
            sendb.at[C - 1, pl.ds(pl.multiple_of((r % RC) * dr, dr), dr)],
            out.at[:, pl.ds(pl.multiple_of(r * kl, kl), kl)],
            lsem.at[1],
        )

    grad_load(0).start()

    def grad(n, _):
        t = n // R

        @pl.when(n + 1 < R * C)
        def _():
            grad_load(n + 1).start()

        grad_load(n).wait()
        part = jnp.dot(SL[n % R], fbuf[n % 2], preferred_element_type=F32)

        @pl.when(n % R == 0)
        def _():
            GT[...] = part

        @pl.when(n % R > 0)
        def _():
            GT[...] += part

        @pl.when(n % R == R - 1)
        def _():
            sendb[t] = GT[...].T.astype(BF16)
            for j in range(RC):

                @pl.when(block_of(t) * RC + j != r)
                def _():
                    grad_copy(t, j, r).start()

                @pl.when(block_of(t) * RC + j == r)
                def _():
                    own_grad().start()

        return 0

    lax.fori_loop(0, R * C, grad, 0)

    def drain(o, _):
        for h in (0, 1):

            @pl.when(jnp.logical_and(o <= z, z + 1 < Z))
            def _():
                line_up(o, h).wait_send()

            @pl.when(jnp.logical_and(o >= z, z >= 1))
            def _():
                line_down(o, h).wait_send()

            near(0, o, h).wait_send()
            near(1, o, h).wait_send()
            diag(h, o).wait_send()
            for quad in range(4):
                pair(quad, o, h).wait_send()

        return 0

    lax.fori_loop(0, Z, drain, 0)
    own_grad().wait()

    def sent(n, _):
        @pl.when(block_of(n // RC) * RC + n % RC != r)
        def _():
            grad_copy(n // RC, n % RC, r).wait_send()

        return 0

    lax.fori_loop(0, C * RC, sent, 0)

    def got(o, _):
        grad_copy(0, 0, rpeer(o)).wait_recv()
        return 0

    lax.fori_loop(1, R, got, 0)


def solution(mesh):
    R, C = mesh.shape["rows"], mesh.shape["cls"]
    assert C == 4 and R % 4 == 0

    def local(features, prototypes):
        Bl, dl = features.shape
        dr, kc = prototypes.shape
        kl = kc // R
        Z, RC = R // 2, R // C
        X = ITERS + 1
        dma = pltpu.SemaphoreType.DMA
        V = pltpu.VMEM
        out, _ = pl.pallas_call(
            functools.partial(kernel, R, C),
            out_shape=(
                jax.ShapeDtypeStruct((dr, kc), BF16),
                jax.ShapeDtypeStruct((R, C, Bl, dl), BF16),
            ),
            in_specs=[pl.BlockSpec(memory_space=pl.ANY)] * 2,
            out_specs=(pl.BlockSpec(memory_space=pl.ANY),) * 2,
            scratch_shapes=[
                V((C, dl, kl), BF16),
                V((C, kl, dl), BF16),
                V((R, kl, Bl), F32),
                V((R, kl, Bl), F32),
                V((R, kl, Bl), BF16),
                V((kl, dl), F32),
                V((4, Bl, dl), BF16),
                V((C, dl, kl), BF16),
                V((R, 3, 1, Bl), F32),
                V((ITERS, R, 1, 1, Bl), F32),
                V((C, RC, 3, 1, Bl), F32),
                V((R, RC, 3, 1, Bl), F32),
                V((ITERS, C, RC, 1, 1, Bl), F32),
                V((ITERS, R, RC, 1, 1, Bl), F32),
                V((RC, 3, 1, Bl), F32),
                V((ITERS, RC, 1, 1, Bl), F32),
                V((R, 3, 1, Bl), F32),
                V((ITERS, R, 1, 1, Bl), F32),
                V((R, 1, Bl), F32),
                V((R, 1, Bl), F32),
                V((R, 1, Bl), F32),
                V((kl, 128), F32),
                dma((6,)),
                dma((4, Z, 2)),
                dma((4, Z, 2)),
                dma((Z, 2)),
                dma((Z, 2)),
                dma((Z, 2)),
                dma((2, Z, 2)),
                dma((2, Z, 2)),
                dma((Z, 2)),
                dma((Z, 2)),
                dma((R,)),
                dma((R,)),
                dma((X, C)),
                dma((X, C)),
                dma((X, R)),
                dma((X, R)),
                dma((X, C)),
                dma((X, C)),
                dma((C, RC)),
                dma((R,)),
            ],
            compiler_params=pltpu.CompilerParams(
                collective_id=0, has_side_effects=True, vmem_limit_bytes=60 * 1024 * 1024
            ),
        )(features, prototypes)
        return out.astype(F32)

    return jax.shard_map(
        local,
        mesh=mesh,
        in_specs=(P("rows", "cls"), P("rows", "cls")),
        out_specs=P("rows", "cls"),
        check_vma=False,
    )
```

```python
import functools

import jax
import jax.numpy as jnp
from jax import lax
from jax.experimental import pallas as pl
from jax.experimental.pallas import tpu as pltpu
from jax.sharding import PartitionSpec as P

ITERS = 3
code_temp = 0.2
loss_temp = 0.3

MESH = pl.DeviceIdType.MESH
F32 = jnp.float32
BF16 = jnp.bfloat16


def kernel(
    R, C, feat, protos, out, G, Pb, PT, S, E, SL, GT, fbuf, sendb, st0, st1, a1, a2, b1, b2, q0, q1, res0, res1, wv, av, fv, cs,
    lsem, ps, pr, up_s, dn_s, ln_r, ns, nr, ds_, dr_, c_s, c_r, x1s, x1r, x2s, x2r, x3s, x3r, gsend, grecv,
):
    Z = R // 2
    RC = R // C
    Bl, dl = feat.shape
    hb = Bl // 2
    dr = protos.shape[0]
    kl = protos.shape[1] // R
    ratio = float(Bl * R) / float(protos.shape[1] * C)

    r = lax.axis_index("rows")
    c = lax.axis_index("cls")
    x, core = c // 2, c % 2
    z, y = r // 2, r % 2
    x_near = (r, (1 - x) * 2 + core)
    y_near = (2 * z + 1 - y, c)
    partner = (r, x * 2 + 1 - core)

    def rpeer(o):
        return (r + o) % R

    def cpeer(o):
        return (c + o) % C

    barrier = pltpu.get_barrier_semaphore()

    def sig_r(o, _):
        pl.semaphore_signal(barrier, inc=1, device_id=(rpeer(o), c), device_id_type=MESH)
        return 0

    def sig_c(o, _):
        pl.semaphore_signal(barrier, inc=1, device_id=(r, cpeer(o)), device_id_type=MESH)
        return 0

    own = pltpu.make_async_copy(feat, G.at[r, c], lsem.at[0])
    own.start()
    lax.fori_loop(1, R, sig_r, 0)
    lax.fori_loop(1, C, sig_c, 0)
    pl.semaphore_wait(barrier, R + C - 2)

    def half(quad, o, h, co):
        xq = 1 - x if quad in (1, 3) else x
        yq = 1 - y if quad in (2, 3) else y
        return G.at[2 * o + yq, 2 * xq + co, pl.ds(h * hb, hb)]

    def send(dst, send_sem, recv_sem, dest, src=None):
        return pltpu.make_async_remote_copy(
            src_ref=dst if src is None else src, dst_ref=dst, send_sem=send_sem, recv_sem=recv_sem, device_id=dest, device_id_type=MESH
        )

    def line_up(o, h, src=None):
        return send(half(0, o, h, core), up_s.at[o, h], ln_r.at[o, h], (r + 2, c), src)

    def line_down(o, h, src=None):
        return send(half(0, o, h, core), dn_s.at[o, h], ln_r.at[o, h], (r - 2, c), src)

    def line_in(o, h):
        return send(half(0, o, h, core), up_s.at[o, h], ln_r.at[o, h], partner)

    def near(axis, o, h, src=None):
        return send(half(0, o, h, core), ns.at[axis, o, h], nr.at[axis, o, h], (x_near, y_near)[axis], src)

    def near_in(axis, o, h):
        return send(half(1 + axis, o, h, core), ns.at[axis, o, h], nr.at[axis, o, h], (x_near, y_near)[axis])

    def diag(h, o):
        return send(half(2 - h, o, h, core), ds_.at[o, h], dr_.at[o, h], (x_near, y_near)[h])

    def diag_in(h, o):
        return send(half(3, o, h, core), ds_.at[o, h], dr_.at[o, h], (x_near, y_near)[h])

    def pair(quad, o, h, src=None):
        return send(half(quad, o, h, core), ps.at[quad, o, h], pr.at[quad, o, h], partner, src)

    def pair_in(quad, o, h):
        return send(half(quad, o, h, 1 - core), ps.at[quad, o, h], pr.at[quad, o, h], partner)

    def sides(k, fn):
        if isinstance(k, int) and k == 0:
            fn(z, None)
            return

        @pl.when(z - k >= 0)
        def _():
            fn(z - k, 0)

        @pl.when(z + k < Z)
        def _():
            fn(z + k, 1)

    def do_line(k):
        def step(o, side):
            for h in (0, 1):
                src = feat.at[pl.ds(h * hb, hb)] if side is None else None
                if side is not None:
                    line_in(o, h).wait_recv()
                if side != 1:

                    @pl.when(z + 1 < Z)
                    def _():
                        line_up(o, h, src).start()

                if side != 0:

                    @pl.when(z >= 1)
                    def _():
                        line_down(o, h, src).start()

                near(0, o, h, src).start()
                near(1, o, h, src).start()
                pair(0, o, h, src).start()

        sides(k, step)

    def do_near(k):
        def step(o, side):
            for h in (0, 1):
                for axis in (1, 0):
                    near_in(axis, o, h).wait_recv()
                    if axis == 1 - h:
                        diag(h, o).start()
                    pair(1 + axis, o, h).start()

        sides(k, step)

    def do_diag(k):
        def step(o, side):
            for h in (0, 1):
                diag_in(h, o).wait_recv()
                pair(3, o, h).start()

        sides(k, step)

    do_line(0)

    def proto_copy(o, slot_r):
        return pltpu.make_async_remote_copy(
            src_ref=protos.at[:, pl.ds(pl.multiple_of(rpeer(o) * kl, kl), kl)],
            dst_ref=Pb.at[slot_r // RC, pl.ds(pl.multiple_of((slot_r % RC) * dr, dr), dr)],
            send_sem=c_s.at[o], recv_sem=c_r.at[o],
            device_id=(rpeer(o), c), device_id_type=MESH,
        )

    def proto_start(o, _):
        proto_copy(o, r).start()
        return 0

    mine = pltpu.make_async_copy(
        protos.at[:, pl.ds(pl.multiple_of(r * kl, kl), kl)],
        Pb.at[r // RC, pl.ds(pl.multiple_of((r % RC) * dr, dr), dr)],
        lsem.at[1],
    )
    mine.start()
    def zero(i, _):
        S[i] = jnp.zeros(S.shape[1:], F32)
        return 0

    lax.fori_loop(0, R, zero, 0)

    def proto_wait(o, _):
        proto_copy(o, (r - o + R) % R).wait()
        return 0

    def turn(i, _):
        PT[i] = Pb[i].astype(F32).T.astype(BF16)
        return 0

    def prepare():
        lax.fori_loop(1, R, proto_wait, 0)
        mine.wait()
        lax.fori_loop(0, C, turn, 0)
        own.wait()

    def load(r_, c_, slot):
        return pltpu.make_async_copy(G.at[r_, c_], fbuf.at[slot], lsem.at[2 + slot])

    def absorb(quads, k):
        def step(o, side):
            blocks = []
            for quad in quads:
                for h in (0, 1):
                    pair_in(quad, o, h).wait_recv()
                xq = 1 - x if quad in (1, 3) else x
                yq = 1 - y if quad in (2, 3) else y
                blocks += [(2 * o + yq, 2 * xq + core), (2 * o + yq, 2 * xq + 1 - core)]
            for i, (r_, c_) in enumerate(blocks):
                load(r_, c_, i).start()
            for i, (r_, c_) in enumerate(blocks):
                load(r_, c_, i).wait()
                S[r_] += lax.dot_general(PT[c_], fbuf[i], (((1,), (1,)), ((), ())), preferred_element_type=F32)

        sides(k, step)

    do_line(1)
    lax.fori_loop(1, R, proto_start, 0)
    do_near(0)

    def later(k, _):
        @pl.when(k < Z)
        def _():
            do_line(k)

        do_near(k - 1)

        @pl.when(k == 2)
        def _():
            do_diag(0)
            prepare()
            absorb((0,), 0)
            absorb((1, 2), 0)
            absorb((3,), 0)

        absorb((0,), k - 1)

        @pl.when(k > 2)
        def _():
            do_diag(k - 2)
            absorb((1, 2), k - 2)
            absorb((3,), k - 2)

        return 0

    lax.fori_loop(2, Z + 1, later, 0)
    absorb((1, 2), Z - 1)
    do_diag(Z - 1)
    absorb((3,), Z - 1)

    def exchange(e, st, s1, s2, qv, res, join):
        def one(o):
            return pltpu.make_async_remote_copy(
                src_ref=st.at[pl.ds(cpeer(o) * RC, RC)], dst_ref=s1.at[c],
                send_sem=x1s.at[e, o], recv_sem=x1r.at[e, o], device_id=(r, cpeer(o)), device_id_type=MESH,
            )

        for o in range(1, C):
            one(o).start()
        s1[c] = st[pl.ds(c * RC, RC)]
        for o in range(1, C):
            one(o).wait()
        qv[...] = join([s1[i] for i in range(C)])

        def two(o):
            return pltpu.make_async_remote_copy(
                src_ref=qv, dst_ref=s2.at[r],
                send_sem=x2s.at[e, o], recv_sem=x2r.at[e, o], device_id=(rpeer(o), c), device_id_type=MESH,
            )

        for o in range(1, R):
            two(o).start()
        s2[r] = qv[...]
        for o in range(1, R):
            two(o).wait()
        res[pl.ds(c * RC, RC)] = join([s2[i] for i in range(R)])

        def three(o):
            return pltpu.make_async_remote_copy(
                src_ref=res.at[pl.ds(c * RC, RC)], dst_ref=res.at[pl.ds(c * RC, RC)],
                send_sem=x3s.at[e, o], recv_sem=x3r.at[e, o], device_id=(r, cpeer(o)), device_id_type=MESH,
            )

        for o in range(1, C):
            three(o).start()
        for o in range(1, C):
            three(o).wait()

    def join_stats(parts):
        top = functools.reduce(jnp.maximum, [p[:, 0] for p in parts])
        s2 = sum(p[:, 1] * jnp.exp((p[:, 0] - top) / code_temp) for p in parts)
        s3 = sum(p[:, 2] * jnp.exp((p[:, 0] - top) / loss_temp) for p in parts)
        return jnp.stack([top, s2, s3], axis=1)

    def join_sum(parts):
        return functools.reduce(jnp.add, parts)

    def first(i, _):
        sc = S[i]
        top = jnp.max(sc, axis=0, keepdims=True)
        sh = sc - top
        e2 = jnp.exp(sh / code_temp)
        e3 = jnp.exp(sh / loss_temp)
        E[i] = e2
        S[i] = e3
        st0[i, 0] = top
        st0[i, 1] = jnp.sum(e2, axis=0, keepdims=True)
        st0[i, 2] = jnp.sum(e3, axis=0, keepdims=True)
        return 0

    lax.fori_loop(0, R, first, 0)
    exchange(0, st0, a1, a2, q0, res0, join_stats)

    def scales(i, _):
        down = st0[i, 0] - res0[i, 0]
        f2 = jnp.exp(down / code_temp)
        fv[i] = f2
        wv[i] = f2 / res0[i, 1]
        av[i] = jnp.exp(down / loss_temp) / res0[i, 2]
        return 0

    lax.fori_loop(0, R, scales, 0)

    for sweep in range(ITERS):

        def col(i, acc):
            m = E[i] * wv[i]
            return acc + functools.reduce(jnp.add, [m[:, j * 128 : (j + 1) * 128] for j in range(Bl // 128)])

        mass = lax.fori_loop(0, R, col, jnp.zeros((kl, 128), F32))
        cs[...] = jnp.broadcast_to(ratio / jnp.sum(mass, axis=1, keepdims=True), (kl, 128))

        def row(i, _):
            st1[sweep, i, 0] = jnp.sum(E[i] * cs[:, 0:1], axis=0, keepdims=True) * fv[i]
            return 0

        lax.fori_loop(0, R, row, 0)
        exchange(sweep + 1, st1.at[sweep], b1.at[sweep], b2.at[sweep], q1.at[sweep], res1.at[sweep], join_sum)

        def rescale(i, _):
            wv[i] = fv[i] / res1[sweep, i, 0]
            return 0

        lax.fori_loop(0, R, rescale, 0)

    def slope(i, _):
        SL[i] = ((S[i] * av[i] - E[i] * wv[i] * cs[:, 0:1]) / loss_temp).astype(BF16)
        return 0

    lax.fori_loop(0, R, slope, 0)

    def block_of(t):
        g = r // RC
        return (2 * (g // 2) + 2 * (1 - t // 2)) % 4 + (g + 1 - t % 2) % 2

    def grad_load(n):
        cb = block_of(n // R)
        return load(n % R, cb, n % 2)

    def grad_copy(t, j, src_r):
        dest = block_of(t) * RC + j
        return pltpu.make_async_remote_copy(
            src_ref=sendb.at[t, pl.ds(pl.multiple_of(j * dr, dr), dr)],
            dst_ref=out.at[:, pl.ds(pl.multiple_of(src_r * kl, kl), kl)],
            send_sem=gsend.at[t, j], recv_sem=grecv.at[src_r],
            device_id=(dest, c), device_id_type=MESH,
        )

    def own_grad():
        return pltpu.make_async_copy(
            sendb.at[C - 1, pl.ds(pl.multiple_of((r % RC) * dr, dr), dr)],
            out.at[:, pl.ds(pl.multiple_of(r * kl, kl), kl)],
            lsem.at[1],
        )

    grad_load(0).start()

    def grad(n, _):
        t = n // R

        @pl.when(n + 1 < R * C)
        def _():
            grad_load(n + 1).start()

        grad_load(n).wait()
        part = jnp.dot(SL[n % R], fbuf[n % 2], preferred_element_type=F32)

        @pl.when(n % R == 0)
        def _():
            GT[...] = part

        @pl.when(n % R > 0)
        def _():
            GT[...] += part

        @pl.when(n % R == R - 1)
        def _():
            sendb[t] = GT[...].T.astype(BF16)
            for j in range(RC):

                @pl.when(block_of(t) * RC + j != r)
                def _():
                    grad_copy(t, j, r).start()

                @pl.when(block_of(t) * RC + j == r)
                def _():
                    own_grad().start()

        return 0

    lax.fori_loop(0, R * C, grad, 0)

    def drain(o, _):
        for h in (0, 1):

            @pl.when(jnp.logical_and(o <= z, z + 1 < Z))
            def _():
                line_up(o, h).wait_send()

            @pl.when(jnp.logical_and(o >= z, z >= 1))
            def _():
                line_down(o, h).wait_send()

            near(0, o, h).wait_send()
            near(1, o, h).wait_send()
            diag(h, o).wait_send()
            for quad in range(4):
                pair(quad, o, h).wait_send()

        return 0

    lax.fori_loop(0, Z, drain, 0)
    own_grad().wait()

    def sent(n, _):
        @pl.when(block_of(n // RC) * RC + n % RC != r)
        def _():
            grad_copy(n // RC, n % RC, r).wait_send()

        return 0

    lax.fori_loop(0, C * RC, sent, 0)

    def got(o, _):
        grad_copy(0, 0, rpeer(o)).wait_recv()
        return 0

    lax.fori_loop(1, R, got, 0)


def solution(mesh):
    R, C = mesh.shape["rows"], mesh.shape["cls"]
    assert C == 4 and R % 4 == 0

    def local(features, prototypes):
        Bl, dl = features.shape
        dr, kc = prototypes.shape
        kl = kc // R
        Z, RC = R // 2, R // C
        X = ITERS + 1
        dma = pltpu.SemaphoreType.DMA
        V = pltpu.VMEM
        out, _ = pl.pallas_call(
            functools.partial(kernel, R, C),
            out_shape=(
                jax.ShapeDtypeStruct((dr, kc), BF16),
                jax.ShapeDtypeStruct((R, C, Bl, dl), BF16),
            ),
            in_specs=[pl.BlockSpec(memory_space=pl.ANY)] * 2,
            out_specs=(pl.BlockSpec(memory_space=pl.ANY),) * 2,
            scratch_shapes=[
                V((C, dl, kl), BF16),
                V((C, kl, dl), BF16),
                V((R, kl, Bl), F32),
                V((R, kl, Bl), F32),
                V((R, kl, Bl), BF16),
                V((kl, dl), F32),
                V((4, Bl, dl), BF16),
                V((C, dl, kl), BF16),
                V((R, 3, 1, Bl), F32),
                V((ITERS, R, 1, 1, Bl), F32),
                V((C, RC, 3, 1, Bl), F32),
                V((R, RC, 3, 1, Bl), F32),
                V((ITERS, C, RC, 1, 1, Bl), F32),
                V((ITERS, R, RC, 1, 1, Bl), F32),
                V((RC, 3, 1, Bl), F32),
                V((ITERS, RC, 1, 1, Bl), F32),
                V((R, 3, 1, Bl), F32),
                V((ITERS, R, 1, 1, Bl), F32),
                V((R, 1, Bl), F32),
                V((R, 1, Bl), F32),
                V((R, 1, Bl), F32),
                V((kl, 128), F32),
                dma((6,)),
                dma((4, Z, 2)),
                dma((4, Z, 2)),
                dma((Z, 2)),
                dma((Z, 2)),
                dma((Z, 2)),
                dma((2, Z, 2)),
                dma((2, Z, 2)),
                dma((Z, 2)),
                dma((Z, 2)),
                dma((R,)),
                dma((R,)),
                dma((X, C)),
                dma((X, C)),
                dma((X, R)),
                dma((X, R)),
                dma((X, C)),
                dma((X, C)),
                dma((C, RC)),
                dma((R,)),
            ],
            compiler_params=pltpu.CompilerParams(
                collective_id=0, has_side_effects=True, vmem_limit_bytes=60 * 1024 * 1024
            ),
        )(features, prototypes)
        return out.astype(F32)

    return jax.shard_map(
        local,
        mesh=mesh,
        in_specs=(P("rows", "cls"), P("rows", "cls")),
        out_specs=P("rows", "cls"),
        check_vma=False,
    )
```
